32 devices in a mesh: wide: 8 (over y, x, core), narrow: 4 (over z).
Axes of the slice: x: 2, y: 2, z: 4, core: 2. Of those that a mesh axis runs over, the one named last changes fastest.
Arguments:
- loads: bfloat16 [256, 262144], P('narrow', 'wide'), may hold values from -6 to 6
- state: bfloat16 [256, 262144], P('narrow', 'wide'), may hold values from -6 to 6
- modal_diag: float32 [262144], P('wide'), may hold values from 0.5 to 2
- phi: bfloat16 [2048, 128, 128], P('wide'), may hold values from -0.25 to 0.25
- incidence: int32 [2048], P('wide'), may hold values from 0 to 127
- sizes: int32 [1024], P('wide'), may hold values from 1 to 129, as said below
- factor: float32 [16384, 16384], P('wide', 'narrow'), may hold values from -0.046875 to 0.046875
Outputs:
- adjoint: bfloat16 [256, 262144], P('narrow', 'wide')
- sensitivity: float32 [256, 1024], P('narrow', 'wide')
The draws below stay inside these ranges and needn't reach their ends.
Inputs may be any that keep to these rules, and one draw needn't show every extreme that they name: `sizes`: the 128 substructures of each group hold at most 256 tiles together, and in every draw some group holds exactly 256.
All inputs are finite; a program needn't handle non-finite values.
Results may differ from the reference program's by a relative error of at most 0.015.
Values may be sent and summed in bfloat16 or wider, within the bound.
A program may use at most 128 MiB of HBM per device.

```python
import math
import jax
import jax.numpy as jnp
from jax import lax

MODES = 16384
BLOCK = 128
LOADS = 256
SUBS_DEV = 128
TILES_DEV = 256
SUBS = 1024
TILES = 2048
ROWS = 262144
MBLOCKS = 128


def draw_sizes(key, part):
    groups = SUBS // SUBS_DEV
    spare = TILES_DEV - SUBS_DEV
    first_key, second_key, third_key, fourth_key = jax.random.split(jax.random.fold_in(key, 7), 4)
    extra = jax.random.randint(first_key, (groups,), 0, spare + 1)
    fullest = jax.random.randint(second_key, (), 0, groups)
    heaviest = jax.random.randint(fourth_key, (), 0, SUBS_DEV)
    is_full = jnp.arange(groups) == fullest
    extra = jnp.where(is_full, spare, extra)
    targets = jax.random.randint(third_key, (groups, spare), 0, SUBS_DEV)
    targets = jnp.where(is_full[:, None], heaviest, targets)
    used = jnp.arange(spare)[None, :] < extra[:, None]
    hits = (targets[:, :, None] == jnp.arange(SUBS_DEV)[None, None, :]) & used[:, :, None]
    counts = jnp.sum(hits.astype(jnp.int32), axis=1)
    return (1 + counts).reshape(groups * SUBS_DEV).astype(jnp.int32)


def with_ends(result, own_key, low, top_value):
    longest = result.shape.index(max(result.shape))
    spots = []
    for shift in (0, 1):
        where = [jax.random.randint(jax.random.fold_in(own_key, axis), (), 0, length) for axis, length in enumerate(result.shape)]
        where[longest] = (where[longest] + shift) % result.shape[longest]
        spots.append(tuple(where))
    return result.at[spots[0]].set(low).at[spots[1]].set(top_value)


def steps_of(key, dims, shards, smallest, top_value):
    level = 1.0
    for position, shards_of in shards:
        steps = jax.random.uniform(jax.random.fold_in(jax.random.fold_in(key, 6), position), (shards_of,), jnp.float32, smallest / len(shards), top_value / len(shards))
        level = level * jnp.repeat(jnp.exp(steps), dims[position] // shards_of).reshape((-1,) + (1,) * (len(dims) - 1 - position))
    return level


def bell_draw(own_key, extent, spread, most, pieces=(), kind=jnp.bfloat16):
    factor_of = steps_of(own_key, extent, pieces, -0.22, 0.18) if pieces else 1.0
    drawn = jax.random.normal(own_key, extent, jnp.float32) * spread * factor_of
    return jnp.minimum(jnp.maximum(drawn, -most), most).astype(kind)


def setup_inputs(seed: int = 0) -> dict:
    keys = jax.random.split(jax.random.key(seed), 8)
    return {
        "loads": bell_draw(keys[0], (LOADS, ROWS), 1.0, 6.0, ((0, 4), (1, 8))),
        "state": bell_draw(keys[1], (LOADS, ROWS), 1.0, 6.0, ((0, 4), (1, 8))),
        "modal_diag": jnp.clip(jnp.exp(math.log(2.0) - 1.3862944 * jax.random.uniform(keys[2], (ROWS,), jnp.float32) ** steps_of(keys[2], (ROWS,), ((0, 8),), -0.2, 0.2)), 0.5, 2.0),
        "phi": bell_draw(keys[3], (TILES, BLOCK, BLOCK), (4 * BLOCK) ** -0.5, 0.25, ((0, 8),)),
        "incidence": with_ends(jax.random.randint(keys[4], (TILES,), 0, MBLOCKS), jax.random.fold_in(keys[4], 1), 0, MBLOCKS - 1).astype(jnp.int32),
        "sizes": draw_sizes(jax.random.fold_in(keys[7], 71), 0),
        "factor": bell_draw(keys[6], (MODES, MODES), MODES ** -0.5, 0.046875, ((0, 8), (1, 4)), jnp.float32),
    }


sens_scale = 0.0625


def reference(loads, state, modal_diag, phi, incidence, sizes, factor):
    groups = SUBS // SUBS_DEV
    block_count = MODES // BLOCK
    load_tiles = loads.reshape(LOADS, groups, TILES_DEV, BLOCK).transpose(1, 0, 2, 3)
    state_tiles = state.reshape(LOADS, groups, TILES_DEV, BLOCK).transpose(1, 0, 2, 3)
    diag_tiles = modal_diag.reshape(groups, TILES_DEV, BLOCK)
    phi_tiles = phi.reshape(groups, TILES_DEV, BLOCK, BLOCK)
    block_ids = incidence.reshape(groups, TILES_DEV)
    group_sizes = sizes.reshape(groups, SUBS_DEV)
    slot_index = jnp.arange(TILES_DEV, dtype=jnp.int32)

    def layout(group_size):
        running = jnp.cumsum(group_size)
        owner_sub = jnp.sum((running[None, :] <= slot_index[:, None]).astype(jnp.int32), axis=1)
        live_slot = slot_index < running[-1]
        return owner_sub, live_slot

    def condense(carry, item):
        load_part, phi_part, id_part, size_part = item
        owner_sub, live_slot = layout(size_part)
        tile_terms = jnp.einsum("lti,tim->tlm", load_part.astype(jnp.float32), phi_part.astype(jnp.float32))
        tile_terms = jnp.where(live_slot[:, None, None], tile_terms, jnp.zeros_like(tile_terms))
        summed = jax.ops.segment_sum(tile_terms, id_part, num_segments=block_count)
        return carry + summed, None

    start_sum = jnp.zeros((block_count, LOADS, BLOCK), jnp.float32)
    blocks_sum, _ = lax.scan(condense, start_sum, (load_tiles, phi_tiles, block_ids, group_sizes))
    condensed = blocks_sum.transpose(1, 0, 2).reshape(LOADS, MODES)
    image = jnp.dot(condensed, factor, precision=lax.Precision.HIGHEST)
    amplitude = jnp.dot(image, factor.T, precision=lax.Precision.HIGHEST)
    amp_round = amplitude.astype(jnp.bfloat16).reshape(LOADS, block_count, BLOCK)

    def recover(item):
        load_part, state_part, diag_part, phi_part, id_part, size_part = item
        owner_sub, live_slot = layout(size_part)
        picked = jnp.take(amp_round, id_part, axis=1).astype(jnp.float32)
        coupling = jnp.einsum("ltm,tim->lti", picked, phi_part.astype(jnp.float32))
        response = diag_part[None, :, :] * load_part.astype(jnp.float32) + coupling
        response = jnp.where(live_slot[None, :, None], response, jnp.zeros_like(response))
        row_totals = jnp.sum(response * state_part.astype(jnp.float32), axis=2) * sens_scale
        member = (owner_sub[:, None] == jnp.arange(SUBS_DEV, dtype=jnp.int32)[None, :]) & live_slot[:, None]
        sensitivity = jnp.dot(row_totals, member.astype(jnp.float32), precision=lax.Precision.HIGHEST)
        return response.astype(jnp.bfloat16), sensitivity

    adjoint_parts, sens_parts = lax.map(recover, (load_tiles, state_tiles, diag_tiles, phi_tiles, block_ids, group_sizes))
    adjoint = adjoint_parts.transpose(1, 0, 2, 3).reshape(LOADS, ROWS)
    sensitivity = sens_parts.transpose(1, 0, 2).reshape(LOADS, SUBS)
    return (adjoint, sensitivity)
```

```python
import functools
import itertools
import jax
import jax.numpy as jnp
from jax import lax
from jax.experimental import pallas as pl
from jax.experimental.pallas import tpu as pltpu
from jax.sharding import PartitionSpec as P

sens_scale = 0.0625
MESH = pl.DeviceIdType.MESH
VMEM_LIMIT = 60 * 1024 * 1024


def condense_kernel(tiles, inc_ref, live_ref, loads_ref, phi_ref, out_ref, acc_ref):
    step = pl.program_id(0)
    width = phi_ref.shape[1]

    @pl.when(step == 0)
    def _():
        acc_ref[...] = jnp.zeros_like(acc_ref)

    for j in range(tiles):
        t = step * tiles + j
        term = jnp.dot(
            loads_ref[:, j * width : (j + 1) * width],
            phi_ref[j],
            preferred_element_type=jnp.float32,
        )
        term = jnp.where(t < live_ref[0], term, jnp.zeros_like(term))
        b = inc_ref[t]
        acc_ref[b] = acc_ref[b] + term

    @pl.when(step == pl.num_programs(0) - 1)
    def _():
        out_ref[...] = acc_ref[...].astype(out_ref.dtype)


def recover_kernel(
    tiles, inc_ref, live_ref, loads_ref, state_ref, diag_ref, phi_ref, amp_ref, first_ref, last_ref,
    adj_ref, sens_ref, acc_ref,
):
    step = pl.program_id(0)
    width = phi_ref.shape[1]

    @pl.when(step == 0)
    def _():
        acc_ref[...] = jnp.zeros_like(acc_ref)

    total = acc_ref[...]
    for j in range(tiles):
        t = step * tiles + j
        cols = slice(j * width, (j + 1) * width)
        coupling = lax.dot_general(
            amp_ref[inc_ref[t]], phi_ref[j], (((1,), (1,)), ((), ())),
            preferred_element_type=jnp.float32,
        )
        response = diag_ref[:, cols] * loads_ref[:, cols].astype(jnp.float32) + coupling
        response = jnp.where(t < live_ref[0], response, jnp.zeros_like(response))
        adj_ref[:, cols] = response.astype(adj_ref.dtype)
        row_total = jnp.sum(response * state_ref[:, cols].astype(jnp.float32), axis=1, keepdims=True)
        member = ((first_ref[...] <= t) & (t < last_ref[...])).astype(jnp.float32)
        total = total + row_total * member
    acc_ref[...] = total

    @pl.when(step == pl.num_programs(0) - 1)
    def _():
        sens_ref[...] = acc_ref[...] * sens_scale


def flips_of(index, size):
    bits = [1 << k for k in range(size.bit_length() - 1)]
    raw = [b * (1 - 2 * ((index // b) % 2)) for b in bits]
    low = index % 2
    rest = raw[1:]
    mixed = [rest[k] + low * (rest[-1 - k] - rest[k]) for k in range(len(rest))]
    return raw, raw[:1] + mixed


def combos(count):
    return list(itertools.product((1, 0), repeat=count))


def slot_of(bits, k, c):
    before = sum(1 << (bits - 1 - j) for j in range(k))
    return before + combos(bits - 1 - k).index(c)


def exchange_kernel(wide, narrow, groups, part_ref, factor_ref, out_ref, *scratch):
    (fac, stage, stage_sem, rs_buf, rs_send, rs_recv, chunk, ag_send, ag_recv,
     amp_part, amp_buf, am_send, am_recv, ow_send, ow_recv, work) = scratch[:16]
    per_group = [scratch[16 + 9 * g : 25 + 9 * g] for g in range(len(groups))]
    own_w, own_n = lax.axis_index("wide"), lax.axis_index("narrow")
    _, flips = flips_of(own_w, wide)
    bits = len(flips)
    narrow_raw, _ = flips_of(own_n, narrow)
    peers = [own_n + sum(narrow_raw[b] for b in range(len(narrow_raw)) if i >> b & 1) for i in range(narrow)]
    partners = [own_w + f for f in flips]
    slots, stage_rows, _ = stage.shape
    stages = factor_ref.shape[0] // stage_rows
    load_rows = part_ref.shape[2]
    width = part_ref.shape[3]

    def load(s):
        return pltpu.make_async_copy(
            factor_ref.at[pl.ds(s * stage_rows, stage_rows)], stage.at[s % slots], stage_sem.at[s % slots]
        )

    for s in range(min(slots, stages)):
        load(s).start()

    barrier = pltpu.get_barrier_semaphore()
    for p in partners:
        pl.semaphore_signal(barrier, inc=1, device_id=(p, own_n), device_id_type=MESH)
    for i in range(1, narrow):
        pl.semaphore_signal(barrier, inc=1, device_id=(own_w, peers[i]), device_id_type=MESH)
    pl.semaphore_wait(barrier, bits + narrow - 1)

    sends = []

    def send(src, dst, ssem, rsem, device):
        copy = pltpu.make_async_remote_copy(
            src_ref=src, dst_ref=dst, send_sem=ssem, recv_sem=rsem, device_id=device, device_id_type=MESH
        )
        copy.start()
        sends.append(copy)
        return copy

    def place(k, c):
        return own_w + sum(flips[k + 1 + j] for j in range(len(c)) if c[j])

    def scatter_send(src, buf, ssem, rsem, k, c):
        slot = slot_of(bits, k, c)
        there = slot_of(bits, k, c[::-1]) if k == 0 else slot
        return send(
            src[min(k, 1)].at[place(k, c) + flips[k]], buf.at[there], ssem.at[slot], rsem.at[there],
            (partners[k], own_n),
        )

    def scatter_wait(buf, ssem, rsem, k, slot):
        pltpu.make_async_remote_copy(
            src_ref=buf.at[slot], dst_ref=buf.at[slot], send_sem=ssem.at[slot], recv_sem=rsem.at[slot],
            device_id=(partners[k], own_n), device_id_type=MESH,
        ).wait_recv()

    def scatter_start(src, buf, ssem, rsem):
        return {c: scatter_send(src, buf, ssem, rsem, 0, c) for c in combos(bits - 1)}

    def scatter_step(src, buf, ssem, rsem, pending, k, finish):
        following = {}
        for c in combos(bits - 1 - k):
            slot = slot_of(bits, k, c)
            scatter_wait(buf, ssem, rsem, k, slot)
            d = place(k, c)
            held = src[min(k, 1)]
            total = (held[d].astype(jnp.float32) + buf[slot].astype(jnp.float32)).astype(held.dtype)
            if k == bits - 1:
                finish(total)
            else:
                src[1][d] = total
                if c[0]:
                    following[c[1:]] = scatter_send(src, buf, ssem, rsem, k + 1, c[1:])
        return following

    def gather_send(buf, ssem, rsem, k):
        pending = []
        for c in combos(bits - 1 - k):
            slot = slot_of(bits, k, c)
            d = place(k, c)
            pending.append(send(buf.at[d], buf.at[d], ssem.at[slot], rsem.at[slot], (partners[k], own_n)))
        return pending

    def convert(lo, hi):
        for s in range(lo, hi):
            load(s).wait()
            rows = stage_rows // 8

            def some(r, carry, s=s):
                here = pl.multiple_of(r * rows, rows)
                fac[pl.ds(s * stage_rows + here, rows), :] = stage[s % slots, pl.ds(here, rows), :].astype(fac.dtype)
                return carry

            lax.fori_loop(0, 8, some, 0)
            if s + slots < stages:
                load(s + slots).start()

    def keep_chunk(total):
        chunk[0] = total

    pending = scatter_start((part_ref, work), rs_buf, rs_send, rs_recv)
    for k in range(bits):
        convert(stages * k // (bits + 1), stages * (k + 1) // (bits + 1))
        pending = scatter_step((part_ref, work), rs_buf, rs_send, rs_recv, pending, k, keep_chunk)
    order = [i for group in groups for i in group]
    chunk_copies = {
        i: send(chunk.at[0], chunk.at[i], ag_send.at[i - 1], ag_recv.at[i - 1], (own_w, peers[i]))
        for i in order if i
    }
    convert(stages * bits // (bits + 1), stages)

    state = [None] * len(groups)
    amp_copies = []

    def run(g, stage_index):
        lhs, lhs2, part, p_buf, p_send, p_recv, image, i_send, i_recv = per_group[g]
        group = groups[g]
        if stage_index == 0:
            for a, i in enumerate(group):
                if i:
                    chunk_copies[i].wait_recv()
                for b in range(chunk.shape[1]):
                    lhs[a * load_rows : (a + 1) * load_rows, b * width : (b + 1) * width] = chunk[i, b]
            cols = part.shape[2]

            def one(d, carry):
                here = pl.multiple_of(d * cols, cols)
                part[d] = jnp.dot(
                    lhs[...], fac[:, pl.ds(here, cols)], preferred_element_type=jnp.float32
                ).astype(part.dtype)
                return carry

            lax.fori_loop(0, wide, one, 0)
            state[g] = scatter_start((part, part), p_buf, p_send, p_recv)
        elif stage_index <= bits:
            def keep(total):
                image[own_w] = total

            state[g] = scatter_step((part, part), p_buf, p_send, p_recv, state[g], stage_index - 1, keep)
            if stage_index == bits:
                state[g] = gather_send(image, i_send, i_recv, bits - 1)
        else:
            k = 2 * bits - stage_index
            for copy in state[g]:
                copy.wait_recv()
            if k > 0:
                state[g] = gather_send(image, i_send, i_recv, k - 1)
                return
            cols = image.shape[2]
            for d in range(wide):
                lhs2[:, d * cols : (d + 1) * cols] = image[d]
            rows = 2 * width

            def two(r, carry):
                here = pl.multiple_of(r * rows, rows)
                value = lax.dot_general(
                    lhs2[...], fac[pl.ds(here, rows), :], (((1,), (1,)), ((), ())),
                    preferred_element_type=jnp.float32,
                ).astype(amp_part.dtype)
                for a, i in enumerate(group):
                    for h in range(2):
                        amp_part[i, 2 * r + h] = value[
                            a * load_rows : (a + 1) * load_rows, h * width : (h + 1) * width
                        ]
                return carry

            lax.fori_loop(0, fac.shape[0] // rows, two, 0)
            for i in group:
                if i:
                    amp_copies.append((i, send(
                        amp_part.at[i], amp_buf.at[i - 1], am_send.at[i - 1], am_recv.at[i - 1],
                        (own_w, peers[i]),
                    )))

    last = 2 * bits
    for tick in range(last + len(groups)):
        for g in range(len(groups)):
            if 0 <= tick - g <= last:
                run(g, tick - g)

    total = amp_part[0].astype(jnp.float32)
    for i, copy in amp_copies:
        copy.wait_recv()
        total = total + amp_buf[i - 1].astype(jnp.float32)
    out_ref[own_w] = total.astype(out_ref.dtype)
    for k in range(bits - 1, -1, -1):
        for copy in gather_send(out_ref, ow_send, ow_recv, k):
            copy.wait_recv()
    for copy in sends:
        copy.wait_send()


def exchange(partial, factor, wide, narrow, groups):
    _, blocks, load_rows, width = partial.shape
    own_rows, own_cols = factor.shape
    cols = own_cols // wide
    bf = partial.dtype
    dma = pltpu.SemaphoreType.DMA
    stage_rows = min(128, own_rows)
    scratch = [
        pltpu.VMEM((own_rows, own_cols), bf),
        pltpu.VMEM((4, stage_rows, own_cols), factor.dtype),
        dma((4,)),
        pltpu.VMEM((wide - 1, blocks, load_rows, width), bf), dma((wide - 1,)), dma((wide - 1,)),
        pltpu.VMEM((narrow, blocks, load_rows, width), bf), dma((narrow - 1,)), dma((narrow - 1,)),
        pltpu.VMEM((narrow, blocks, load_rows, width), bf),
        pltpu.VMEM((narrow - 1, blocks, load_rows, width), bf), dma((narrow - 1,)), dma((narrow - 1,)),
        dma((wide - 1,)), dma((wide - 1,)),
        pltpu.VMEM(partial.shape, bf),
    ]
    for group in groups:
        rows = len(group) * load_rows
        scratch += [
            pltpu.VMEM((rows, own_rows), bf), pltpu.VMEM((rows, own_cols), bf),
            pltpu.VMEM((wide, rows, cols), bf),
            pltpu.VMEM((wide - 1, rows, cols), bf), dma((wide - 1,)), dma((wide - 1,)),
            pltpu.VMEM((wide, rows, cols), bf), dma((wide - 1,)), dma((wide - 1,)),
        ]
    return pl.pallas_call(
        functools.partial(exchange_kernel, wide, narrow, groups),
        out_shape=jax.ShapeDtypeStruct(partial.shape, bf),
        in_specs=[pl.BlockSpec(memory_space=pltpu.VMEM), pl.BlockSpec(memory_space=pl.ANY)],
        out_specs=pl.BlockSpec(memory_space=pltpu.VMEM),
        scratch_shapes=scratch,
        compiler_params=pltpu.CompilerParams(
            collective_id=0, has_side_effects=True, vmem_limit_bytes=VMEM_LIMIT
        ),
        name="exchange",
    )(partial, factor)


def groups_of(narrow):
    order = [0] + list(range(narrow - 1, 0, -1))
    size = max(1, narrow // 2)
    return [order[k : k + size] for k in range(0, narrow, size)]


def body(loads, state, modal_diag, phi, incidence, sizes, factor):
    load_cols = loads.shape[0]
    tile_count, width, _ = phi.shape
    subs_local = sizes.shape[0]
    wide, narrow = lax.axis_size("wide"), lax.axis_size("narrow")
    own_blocks = factor.shape[0] // width
    block_count = own_blocks * wide
    running = jnp.cumsum(sizes)
    live = running[-1:]
    tiles = min(16, tile_count)
    steps = tile_count // tiles
    params = pltpu.CompilerParams(dimension_semantics=("arbitrary",), vmem_limit_bytes=VMEM_LIMIT)
    row_spec = pl.BlockSpec((load_cols, tiles * width), lambda s, *_: (0, s))
    phi_spec = pl.BlockSpec((tiles, width, width), lambda s, *_: (s, 0, 0))
    amp_spec = pl.BlockSpec((block_count, load_cols, width), lambda s, *_: (0, 0, 0))
    sub_spec = pl.BlockSpec((1, subs_local), lambda s, *_: (0, 0))
    sens_spec = pl.BlockSpec((load_cols, subs_local), lambda s, *_: (0, 0))

    partial = pl.pallas_call(
        functools.partial(condense_kernel, tiles),
        out_shape=jax.ShapeDtypeStruct((block_count, load_cols, width), jnp.bfloat16),
        grid_spec=pltpu.PrefetchScalarGridSpec(
            num_scalar_prefetch=2, grid=(steps,), in_specs=[row_spec, phi_spec], out_specs=amp_spec,
            scratch_shapes=[pltpu.VMEM((block_count, load_cols, width), jnp.float32)],
        ),
        compiler_params=params,
        name="condense",
    )(incidence, live, loads, phi)
    amp = exchange(
        partial.reshape(wide, own_blocks, load_cols, width), factor, wide, narrow, groups_of(narrow)
    ).reshape(block_count, load_cols, width)
    adjoint, sensitivity = pl.pallas_call(
        functools.partial(recover_kernel, tiles),
        out_shape=(
            jax.ShapeDtypeStruct(loads.shape, jnp.bfloat16),
            jax.ShapeDtypeStruct((load_cols, subs_local), jnp.float32),
        ),
        grid_spec=pltpu.PrefetchScalarGridSpec(
            num_scalar_prefetch=2, grid=(steps,),
            in_specs=[
                row_spec, row_spec, pl.BlockSpec((1, tiles * width), lambda s, *_: (0, s)),
                phi_spec, amp_spec, sub_spec, sub_spec,
            ],
            out_specs=(row_spec, sens_spec),
            scratch_shapes=[pltpu.VMEM((load_cols, subs_local), jnp.float32)],
        ),
        compiler_params=params,
        name="recover",
    )(
        incidence, live, loads, state, modal_diag.reshape(1, -1), phi, amp,
        (running - sizes).reshape(1, -1), running.reshape(1, -1),
    )
    return (adjoint, sensitivity)


def solution(mesh):
    return jax.shard_map(
        body,
        mesh=mesh,
        in_specs=(
            P("narrow", "wide"),
            P("narrow", "wide"),
            P("wide"),
            P("wide", None, None),
            P("wide"),
            P("wide"),
            P("wide", "narrow"),
        ),
        out_specs=(P("narrow", "wide"), P("narrow", "wide")),
        check_vma=False,
    )
```

```python
import functools
import itertools
import jax
import jax.numpy as jnp
from jax import lax
from jax.experimental import pallas as pl
from jax.experimental.pallas import tpu as pltpu
from jax.sharding import PartitionSpec as P

sens_scale = 0.0625
MESH = pl.DeviceIdType.MESH
VMEM_LIMIT = 60 * 1024 * 1024
STEP_TILES = 64


def condense_kernel(tiles, inc_ref, live_ref, loads_ref, phi_ref, out_ref, acc_ref):
    step = pl.program_id(0)
    width = phi_ref.shape[1]

    @pl.when(step == 0)
    def _():
        acc_ref[...] = jnp.zeros_like(acc_ref)

    for j in range(tiles):
        t = step * tiles + j
        term = jnp.dot(
            loads_ref[:, j * width : (j + 1) * width],
            phi_ref[j],
            preferred_element_type=jnp.float32,
        )
        term = jnp.where(t < live_ref[0], term, jnp.zeros_like(term))
        b = inc_ref[t]
        acc_ref[b] = acc_ref[b] + term

    @pl.when(step == pl.num_programs(0) - 1)
    def _():
        out_ref[...] = acc_ref[...].astype(out_ref.dtype)


def recover_kernel(
    tiles, inc_ref, live_ref, loads_ref, state_ref, diag_ref, phi_ref, amp_ref, first_ref, last_ref,
    adj_ref, sens_ref, acc_ref,
):
    step = pl.program_id(0)
    width = phi_ref.shape[1]

    @pl.when(step == 0)
    def _():
        acc_ref[...] = jnp.zeros_like(acc_ref)

    total = acc_ref[...]
    for j in range(tiles):
        t = step * tiles + j
        cols = slice(j * width, (j + 1) * width)
        coupling = lax.dot_general(
            amp_ref[inc_ref[t]], phi_ref[j], (((1,), (1,)), ((), ())),
            preferred_element_type=jnp.float32,
        )
        response = diag_ref[:, cols] * loads_ref[:, cols].astype(jnp.float32) + coupling
        response = jnp.where(t < live_ref[0], response, jnp.zeros_like(response))
        adj_ref[:, cols] = response.astype(adj_ref.dtype)
        row_total = jnp.sum(response * state_ref[:, cols].astype(jnp.float32), axis=1, keepdims=True)
        member = ((first_ref[...] <= t) & (t < last_ref[...])).astype(jnp.float32)
        total = total + row_total * member
    acc_ref[...] = total

    @pl.when(step == pl.num_programs(0) - 1)
    def _():
        sens_ref[...] = acc_ref[...] * sens_scale


def flips_of(index, size):
    bits = [1 << k for k in range(size.bit_length() - 1)]
    raw = [b * (1 - 2 * ((index // b) % 2)) for b in bits]
    low = index % 2
    rest = raw[1:]
    mixed = [rest[k] + low * (rest[-1 - k] - rest[k]) for k in range(len(rest))]
    return raw, raw[:1] + mixed


def combos(count):
    return list(itertools.product((1, 0), repeat=count))


def slot_of(bits, k, c):
    before = sum(1 << (bits - 1 - j) for j in range(k))
    return before + combos(bits - 1 - k).index(c)


def exchange_kernel(wide, narrow, groups, part_ref, factor_ref, out_ref, *scratch):
    (fac, stage, stage_sem, rs_buf, rs_send, rs_recv, chunk, ag_send, ag_recv,
     amp_part, amp_buf, am_send, am_recv, ow_send, ow_recv, work) = scratch[:16]
    per_group = [scratch[16 + 9 * g : 25 + 9 * g] for g in range(len(groups))]
    own_w, own_n = lax.axis_index("wide"), lax.axis_index("narrow")
    _, flips = flips_of(own_w, wide)
    bits = len(flips)
    narrow_raw, _ = flips_of(own_n, narrow)
    peers = [own_n + sum(narrow_raw[b] for b in range(len(narrow_raw)) if i >> b & 1) for i in range(narrow)]
    partners = [own_w + f for f in flips]
    slots, stage_rows, _ = stage.shape
    stages = factor_ref.shape[0] // stage_rows
    load_rows = part_ref.shape[2]
    width = part_ref.shape[3]

    def load(s):
        return pltpu.make_async_copy(
            factor_ref.at[pl.ds(s * stage_rows, stage_rows)], stage.at[s % slots], stage_sem.at[s % slots]
        )

    for s in range(min(slots, stages)):
        load(s).start()

    barrier = pltpu.get_barrier_semaphore()
    for p in partners:
        pl.semaphore_signal(barrier, inc=1, device_id=(p, own_n), device_id_type=MESH)
    for i in range(1, narrow):
        pl.semaphore_signal(barrier, inc=1, device_id=(own_w, peers[i]), device_id_type=MESH)
    pl.semaphore_wait(barrier, bits + narrow - 1)

    sends = []

    def send(src, dst, ssem, rsem, device):
        copy = pltpu.make_async_remote_copy(
            src_ref=src, dst_ref=dst, send_sem=ssem, recv_sem=rsem, device_id=device, device_id_type=MESH
        )
        copy.start()
        sends.append(copy)
        return copy

    def place(k, c):
        return own_w + sum(flips[k + 1 + j] for j in range(len(c)) if c[j])

    def scatter_send(src, buf, ssem, rsem, k, c):
        slot = slot_of(bits, k, c)
        there = slot_of(bits, k, c[::-1]) if k == 0 else slot
        return send(
            src[min(k, 1)].at[place(k, c) + flips[k]], buf.at[there], ssem.at[slot], rsem.at[there],
            (partners[k], own_n),
        )

    def scatter_wait(buf, ssem, rsem, k, slot):
        pltpu.make_async_remote_copy(
            src_ref=buf.at[slot], dst_ref=buf.at[slot], send_sem=ssem.at[slot], recv_sem=rsem.at[slot],
            device_id=(partners[k], own_n), device_id_type=MESH,
        ).wait_recv()

    def scatter_start(src, buf, ssem, rsem):
        return {c: scatter_send(src, buf, ssem, rsem, 0, c) for c in combos(bits - 1)}

    def scatter_step(src, buf, ssem, rsem, pending, k, finish):
        following = {}
        for c in combos(bits - 1 - k):
            slot = slot_of(bits, k, c)
            scatter_wait(buf, ssem, rsem, k, slot)
            d = place(k, c)
            held = src[min(k, 1)]
            total = (held[d].astype(jnp.float32) + buf[slot].astype(jnp.float32)).astype(held.dtype)
            if k == bits - 1:
                finish(total)
            else:
                src[1][d] = total
                if c[0]:
                    following[c[1:]] = scatter_send(src, buf, ssem, rsem, k + 1, c[1:])
        return following

    def gather_send(buf, ssem, rsem, k):
        pending = []
        for c in combos(bits - 1 - k):
            slot = slot_of(bits, k, c)
            d = place(k, c)
            pending.append(send(buf.at[d], buf.at[d], ssem.at[slot], rsem.at[slot], (partners[k], own_n)))
        return pending

    def convert(lo, hi):
        for s in range(lo, hi):
            load(s).wait()
            rows = stage_rows // 8

            def some(r, carry, s=s):
                here = pl.multiple_of(r * rows, rows)
                fac[pl.ds(s * stage_rows + here, rows), :] = stage[s % slots, pl.ds(here, rows), :].astype(fac.dtype)
                return carry

            lax.fori_loop(0, 8, some, 0)
            if s + slots < stages:
                load(s + slots).start()

    def keep_chunk(total):
        chunk[0] = total

    pending = scatter_start((part_ref, work), rs_buf, rs_send, rs_recv)
    for k in range(bits):
        convert(stages * k // (bits + 1), stages * (k + 1) // (bits + 1))
        pending = scatter_step((part_ref, work), rs_buf, rs_send, rs_recv, pending, k, keep_chunk)
    order = [i for group in groups for i in group]
    chunk_copies = {
        i: send(chunk.at[0], chunk.at[i], ag_send.at[i - 1], ag_recv.at[i - 1], (own_w, peers[i]))
        for i in order if i
    }
    convert(stages * bits // (bits + 1), stages)

    state = [None] * len(groups)
    amp_copies = []

    def run(g, stage_index):
        lhs, lhs2, part, p_buf, p_send, p_recv, image, i_send, i_recv = per_group[g]
        group = groups[g]
        if stage_index == 0:
            for a, i in enumerate(group):
                if i:
                    chunk_copies[i].wait_recv()
                for b in range(chunk.shape[1]):
                    lhs[a * load_rows : (a + 1) * load_rows, b * width : (b + 1) * width] = chunk[i, b]
            cols = part.shape[2]

            def one(d, carry):
                here = pl.multiple_of(d * cols, cols)
                part[d] = jnp.dot(
                    lhs[...], fac[:, pl.ds(here, cols)], preferred_element_type=jnp.float32
                ).astype(part.dtype)
                return carry

            lax.fori_loop(0, wide, one, 0)
            state[g] = scatter_start((part, part), p_buf, p_send, p_recv)
        elif stage_index <= bits:
            def keep(total):
                image[own_w] = total

            state[g] = scatter_step((part, part), p_buf, p_send, p_recv, state[g], stage_index - 1, keep)
            if stage_index == bits:
                state[g] = gather_send(image, i_send, i_recv, bits - 1)
        else:
            k = 2 * bits - stage_index
            for copy in state[g]:
                copy.wait_recv()
            if k > 0:
                state[g] = gather_send(image, i_send, i_recv, k - 1)
                return
            cols = image.shape[2]
            for d in range(wide):
                lhs2[:, d * cols : (d + 1) * cols] = image[d]
            rows = 2 * width

            def two(r, carry):
                here = pl.multiple_of(r * rows, rows)
                value = lax.dot_general(
                    lhs2[...], fac[pl.ds(here, rows), :], (((1,), (1,)), ((), ())),
                    preferred_element_type=jnp.float32,
                ).astype(amp_part.dtype)
                for a, i in enumerate(group):
                    for h in range(2):
                        amp_part[i, 2 * r + h] = value[
                            a * load_rows : (a + 1) * load_rows, h * width : (h + 1) * width
                        ]
                return carry

            lax.fori_loop(0, fac.shape[0] // rows, two, 0)
            for i in group:
                if i:
                    amp_copies.append((i, send(
                        amp_part.at[i], amp_buf.at[i - 1], am_send.at[i - 1], am_recv.at[i - 1],
                        (own_w, peers[i]),
                    )))

    last = 2 * bits
    for tick in range(last + len(groups)):
        for g in range(len(groups)):
            if 0 <= tick - g <= last:
                run(g, tick - g)

    total = amp_part[0].astype(jnp.float32)
    for i, copy in amp_copies:
        copy.wait_recv()
        total = total + amp_buf[i - 1].astype(jnp.float32)
    out_ref[own_w] = total.astype(out_ref.dtype)
    for k in range(bits - 1, -1, -1):
        for copy in gather_send(out_ref, ow_send, ow_recv, k):
            copy.wait_recv()
    for copy in sends:
        copy.wait_send()


def exchange(partial, factor, wide, narrow, groups):
    _, blocks, load_rows, width = partial.shape
    own_rows, own_cols = factor.shape
    cols = own_cols // wide
    bf = partial.dtype
    dma = pltpu.SemaphoreType.DMA
    stage_rows = min(128, own_rows)
    scratch = [
        pltpu.VMEM((own_rows, own_cols), bf),
        pltpu.VMEM((4, stage_rows, own_cols), factor.dtype),
        dma((4,)),
        pltpu.VMEM((wide - 1, blocks, load_rows, width), bf), dma((wide - 1,)), dma((wide - 1,)),
        pltpu.VMEM((narrow, blocks, load_rows, width), bf), dma((narrow - 1,)), dma((narrow - 1,)),
        pltpu.VMEM((narrow, blocks, load_rows, width), bf),
        pltpu.VMEM((narrow - 1, blocks, load_rows, width), bf), dma((narrow - 1,)), dma((narrow - 1,)),
        dma((wide - 1,)), dma((wide - 1,)),
        pltpu.VMEM(partial.shape, bf),
    ]
    for group in groups:
        rows = len(group) * load_rows
        scratch += [
            pltpu.VMEM((rows, own_rows), bf), pltpu.VMEM((rows, own_cols), bf),
            pltpu.VMEM((wide, rows, cols), bf),
            pltpu.VMEM((wide - 1, rows, cols), bf), dma((wide - 1,)), dma((wide - 1,)),
            pltpu.VMEM((wide, rows, cols), bf), dma((wide - 1,)), dma((wide - 1,)),
        ]
    return pl.pallas_call(
        functools.partial(exchange_kernel, wide, narrow, groups),
        out_shape=jax.ShapeDtypeStruct(partial.shape, bf),
        in_specs=[pl.BlockSpec(memory_space=pltpu.VMEM), pl.BlockSpec(memory_space=pl.ANY)],
        out_specs=pl.BlockSpec(memory_space=pltpu.VMEM),
        scratch_shapes=scratch,
        compiler_params=pltpu.CompilerParams(
            collective_id=0, has_side_effects=True, vmem_limit_bytes=VMEM_LIMIT
        ),
        name="exchange",
    )(partial, factor)


def groups_of(narrow):
    order = [0] + list(range(narrow - 1, 0, -1))
    size = max(1, narrow // 2)
    return [order[k : k + size] for k in range(0, narrow, size)]


def body(loads, state, modal_diag, phi, incidence, sizes, factor):
    load_cols = loads.shape[0]
    tile_count, width, _ = phi.shape
    subs_local = sizes.shape[0]
    wide, narrow = lax.axis_size("wide"), lax.axis_size("narrow")
    own_blocks = factor.shape[0] // width
    block_count = own_blocks * wide
    running = jnp.cumsum(sizes)
    live = running[-1:]
    tiles = min(STEP_TILES, tile_count)
    steps = tile_count // tiles
    params = pltpu.CompilerParams(dimension_semantics=("arbitrary",), vmem_limit_bytes=VMEM_LIMIT)
    row_spec = pl.BlockSpec((load_cols, tiles * width), lambda s, *_: (0, s))
    phi_spec = pl.BlockSpec((tiles, width, width), lambda s, *_: (s, 0, 0))
    amp_spec = pl.BlockSpec((block_count, load_cols, width), lambda s, *_: (0, 0, 0))
    sub_spec = pl.BlockSpec((1, subs_local), lambda s, *_: (0, 0))
    sens_spec = pl.BlockSpec((load_cols, subs_local), lambda s, *_: (0, 0))

    partial = pl.pallas_call(
        functools.partial(condense_kernel, tiles),
        out_shape=jax.ShapeDtypeStruct((block_count, load_cols, width), jnp.bfloat16),
        grid_spec=pltpu.PrefetchScalarGridSpec(
            num_scalar_prefetch=2, grid=(steps,), in_specs=[row_spec, phi_spec], out_specs=amp_spec,
            scratch_shapes=[pltpu.VMEM((block_count, load_cols, width), jnp.float32)],
        ),
        compiler_params=params,
        name="condense",
    )(incidence, live, loads, phi)
    amp = exchange(
        partial.reshape(wide, own_blocks, load_cols, width), factor, wide, narrow, groups_of(narrow)
    ).reshape(block_count, load_cols, width)
    adjoint, sensitivity = pl.pallas_call(
        functools.partial(recover_kernel, tiles),
        out_shape=(
            jax.ShapeDtypeStruct(loads.shape, jnp.bfloat16),
            jax.ShapeDtypeStruct((load_cols, subs_local), jnp.float32),
        ),
        grid_spec=pltpu.PrefetchScalarGridSpec(
            num_scalar_prefetch=2, grid=(steps,),
            in_specs=[
                row_spec, row_spec, pl.BlockSpec((1, tiles * width), lambda s, *_: (0, s)),
                phi_spec, amp_spec, sub_spec, sub_spec,
            ],
            out_specs=(row_spec, sens_spec),
            scratch_shapes=[pltpu.VMEM((load_cols, subs_local), jnp.float32)],
        ),
        compiler_params=params,
        name="recover",
    )(
        incidence, live, loads, state, modal_diag.reshape(1, -1), phi, amp,
        (running - sizes).reshape(1, -1), running.reshape(1, -1),
    )
    return (adjoint, sensitivity)


def solution(mesh):
    return jax.shard_map(
        body,
        mesh=mesh,
        in_specs=(
            P("narrow", "wide"),
            P("narrow", "wide"),
            P("wide"),
            P("wide", None, None),
            P("wide"),
            P("wide"),
            P("wide", "narrow"),
        ),
        out_specs=(P("narrow", "wide"), P("narrow", "wide")),
        check_vma=False,
    )
```
